128 devices in a mesh: replica: 16 (over z_lo, x, core), shard: 8 (over y, z_hi).
Axes of the slice: x: 4, y: 4, z: 4 (z_hi: 2, z_lo: 2; z = z_hi * 2 + z_lo), core: 2. Of those that a mesh axis runs over, the one named last changes fastest.
Arguments:
- params: float32 [16, 128, 28672], P('replica', 'shard'), may hold values from -6 to 6
- first_moment: float32 [16, 128, 28672], P('replica', 'shard'), may hold values from -3 to 3
- second_moment: float32 [16, 128, 28672], P('replica', 'shard'), may hold values from 0.25 to 4
- grads: bfloat16 [4, 16, 128, 28672], P(None, 'replica', 'shard'), may hold values from -6 to 6
- push_weight: float32 [16], P('replica'), may hold values from 0.5 to 2
Outputs:
- final_weights: bfloat16 [16, 128, 28672], P('replica')
The draws below stay inside these ranges and needn't reach their ends.
All inputs are finite; a program needn't handle non-finite values.
Results may differ from the reference program's by a relative error of at most 0.001.
Values may be sent and summed in bfloat16 or wider, within the bound.
No kernel may reach another device: no remote copies, remote signals or barrier semaphores. Data moves between devices by JAX's collectives and lax.ppermute only.
A program may use at most 64 MiB of HBM per device.

```python
import math
import jax
import jax.numpy as jnp

COLS = 28672
STEPS = 4
ROWS = 128
REPLICAS = 16


def steps_of(key, shape, pieces, low, top_value):
    level, own = 1.0, jax.random.fold_in(key, 6)
    for dim, blocks in pieces:
        draws = jnp.exp(jax.random.uniform(jax.random.fold_in(own, dim), (blocks,), jnp.float32, low / len(pieces), top_value / len(pieces)))
        level = level * jnp.repeat(draws, shape[dim] // blocks).reshape([-1 if axis == dim else 1 for axis in range(len(shape))])
    return level


def scatter_about(key, dims, spread, most, cuts=(), held_as=jnp.bfloat16):
    level = steps_of(key, dims, cuts, -0.22, 0.18) if cuts else 1.0
    array = jax.random.normal(key, dims, jnp.float32) * spread * level
    return jnp.minimum(jnp.maximum(array, -most), most).astype(held_as)


def setup_inputs(seed: int = 0) -> dict:
    key_list = jax.random.split(jax.random.key(seed), 6)
    return {
        "params": scatter_about(key_list[0], (REPLICAS, ROWS, COLS), 1.0, 6.0, ((0, 16), (1, 8)), jnp.float32),
        "first_moment": scatter_about(key_list[1], (REPLICAS, ROWS, COLS), 0.5, 3.0, ((0, 16), (1, 8)), jnp.float32),
        "second_moment": jnp.clip(jnp.exp(math.log(4.0) - 2.7725887 * jax.random.uniform(key_list[2], (REPLICAS, ROWS, COLS), jnp.float32) ** steps_of(key_list[2], (REPLICAS, ROWS, COLS), ((0, 16), (1, 8)), -0.2, 0.2)), 0.25, 4.0),
        "grads": scatter_about(key_list[3], (STEPS, REPLICAS, ROWS, COLS), 1.0, 6.0, ((1, 16), (2, 8))),
        "push_weight": jnp.clip(0.5 + 1.5 * jax.random.uniform(key_list[4], (REPLICAS,), jnp.float32) ** steps_of(key_list[4], (REPLICAS,), ((0, 16),), -0.2, 0.2), 0.5, 2.0),
    }


beta_one = 0.9
beta_two = 0.95
learn_rate = 0.1
decay_rate = 0.1
epsilon = 1e-08
adam_offset = 101

def reference(params, first_moment, second_moment, grads, push_weight):
    levels = REPLICAS.bit_length() - 1
    weight = push_weight
    numer = params * weight[:, None, None]
    for iteration in range(STEPS):
        distance = 2 ** (iteration % levels)
        count = adam_offset + iteration
        first_fix = 1.0 - beta_one ** count
        second_fix = 1.0 - beta_two ** count
        current = numer / weight[:, None, None]
        gradient = grads[iteration].astype(jnp.float32)
        first_moment = beta_one * first_moment + (1.0 - beta_one) * gradient
        second_moment = beta_two * second_moment + (1.0 - beta_two) * gradient * gradient
        update = first_moment / first_fix / (jnp.sqrt(second_moment / second_fix) + epsilon)
        current = current - learn_rate * (update + decay_rate * current)
        numer = current * weight[:, None, None]
        numer = 0.5 * numer + 0.5 * jnp.roll(numer, distance, axis=0)
        weight = 0.5 * weight + 0.5 * jnp.roll(weight, distance, axis=0)
    return (numer / weight[:, None, None]).astype(jnp.bfloat16)
```

```python
import jax
import jax.numpy as jnp
import numpy as np
from jax import lax
from jax.sharding import PartitionSpec as P

STEPS = 4
REPLICAS = 16
beta_one = 0.9
beta_two = 0.95
learn_rate = 0.1
decay_rate = 0.1
epsilon = 1e-08
adam_offset = 101

AXES = ("replica", "shard")
DIMS = (2, 4, 2, 4, 2)


def moved(value, to):
    pairs = []
    for place in np.ndindex(*DIMS):
        z_lo, x, core, y, z_hi = place
        x, y, z, core = to(x, y, 2 * z_hi + z_lo, core)
        x, y, z = x % 4, y % 4, z % 4
        target = (z % 2, x, core, y, z // 2)
        pairs.append((int(np.ravel_multi_index(place, DIMS)), int(np.ravel_multi_index(target, DIMS))))
    return lax.ppermute(value, AXES, pairs)


def updates(first_moment, second_moment, grads):
    out = []
    for step in range(STEPS):
        count = adam_offset + step
        gradient = grads[step].astype(jnp.float32)
        first_moment = beta_one * first_moment + (1.0 - beta_one) * gradient
        second_moment = beta_two * second_moment + (1.0 - beta_two) * gradient * gradient
        first_fix = 1.0 - beta_one**count
        second_fix = 1.0 - beta_two**count
        out.append(first_moment / first_fix / (jnp.sqrt(second_moment / second_fix) + epsilon))
    return out


POWER = 15


def coded(value, bound):
    value = value * (2.0**8.5 / bound)
    second = value * value
    fourth = second * second
    return (value * second * fourth * (fourth * fourth)).astype(jnp.bfloat16)


def decoded(code, bound):
    code = code.astype(jnp.float32)
    root = jnp.exp(jnp.log(jnp.abs(code)) * (1.0 / POWER)) * (bound / 2.0**8.5)
    return jnp.where(code < 0, -root, root)


def gathered(piece, y, z):
    rows, cols = piece.shape
    half = cols // 2
    one, two = piece[:, :half], piece[:, half:]
    core = lax.axis_index("replica") % 2
    way = 1 - 2 * core
    along_y = lambda v: moved(v, lambda x, yy, zz, c: (x, yy + 1 - 2 * c, zz, c))
    along_z = lambda v: moved(v, lambda x, yy, zz, c: (x, yy, zz + 1 - 2 * c, c))
    out = jnp.zeros((4, 4, rows, cols), piece.dtype)

    def put(out, part, y_back, z_back, at):
        return lax.dynamic_update_slice(out, part[None, None], ((y - y_back * way) % 4, (z - z_back * way) % 4, 0, at))

    ones, twos = [one], [two]
    for step in range(1, 4):
        ones.append(along_y(ones[-1]))
        twos.append(along_z(twos[-1]))
    for group in ((0,), (1, 2), (3,)):
        block_one = jnp.concatenate([ones[k] for k in group]) if len(group) > 1 else ones[group[0]]
        block_two = jnp.concatenate([twos[k] for k in group]) if len(group) > 1 else twos[group[0]]
        for step in range(4):
            if step:
                block_one = along_z(block_one)
                block_two = along_y(block_two)
            for at, k in enumerate(group):
                out = put(out, block_one[rows * at : rows * at + rows], k, step, 0)
                out = put(out, block_two[rows * at : rows * at + rows], step, k, half)
    return out


def per_device(params, first_moment, second_moment, grads, push_weight):
    replica = lax.axis_index("replica")
    shard = lax.axis_index("shard")
    z_lo, y, z = replica // 8, shard // 2, 2 * (shard % 2) + replica // 8
    cols = params.shape[-1]
    keep = 1.0 - learn_rate * decay_rate

    behind = lambda v, steps: lax.ppermute(v, "replica", [(r, (r + steps) % REPLICAS) for r in range(REPLICAS)])
    one_behind = behind(push_weight, 1)
    four = push_weight + one_behind + behind(push_weight, 2) + behind(push_weight, 3)
    eight = four + behind(four, 4)
    sixteen = eight + behind(four, 8) + behind(four, 12)
    means = [v[0] for v in (push_weight, (push_weight + one_behind) / 2, four / 4, eight / 8, sixteen / 16)]

    halves = lambda v: v.reshape(2, 8, cols)
    u = [halves(v) for v in updates(first_moment[0], second_moment[0], grads[:, 0])]
    a = (keep**4 * halves(params[0]) - learn_rate * keep**3 * u[0]) * (push_weight[0] / 16.0)
    b = (-learn_rate * keep**2 / 8.0 * means[1]) * u[1]
    c = (-learn_rate * keep / 4.0 * means[2]) * u[2]
    d = (-learn_rate / 2.0 * means[3]) * u[3]

    mine = lambda v: jnp.where(z_lo == 0, v[0], v[1])
    other = lambda v: jnp.where(z_lo == 0, v[1], v[0])
    cores = lambda v: moved(v, lambda x, yy, zz, cc: (x, yy, zz, cc ^ 1))

    sent = lambda v, bound, to: decoded(moved(coded(v, bound), to), bound)
    out_a, own_a = other(a), mine(a)
    ab = mine(b) + own_a + cores(own_a) + sent(other(b) + out_a + cores(out_a), 2.0, lambda x, yy, zz, cc: (x, yy, zz ^ 1, cc))
    cz = mine(c) + sent(other(c), 0.5, lambda x, yy, zz, cc: (x, yy, zz ^ 1, cc))
    dz = mine(d) + sent(other(d), 1.0, lambda x, yy, zz, cc: (x, yy, zz ^ 1, cc))
    left, right = ab[:, : cols // 2], ab[:, cols // 2 :]
    left = left + sent(left, 4.0, lambda x, yy, zz, cc: (x ^ 1, yy, zz, cc))
    right = right + sent(right, 4.0, lambda x, yy, zz, cc: (3 - x, yy, zz, cc))
    total = jnp.concatenate([left, right], axis=1) + cz
    total = total + sent(total, 8.0, lambda x, yy, zz, cc: (x ^ 2, yy, zz, cc)) + dz
    piece = (total / means[4]).astype(jnp.bfloat16)
    return gathered(piece, y, z).reshape(1, 128, cols)


def solution(mesh):
    return jax.shard_map(
        per_device,
        mesh=mesh,
        in_specs=(
            P("replica", "shard", None),
            P("replica", "shard", None),
            P("replica", "shard", None),
            P(None, "replica", "shard", None),
            P("replica"),
        ),
        out_specs=P("replica", None, None),
        check_vma=False,
    )
```

```python
import jax
import jax.numpy as jnp
import numpy as np
from jax import lax
from jax.experimental import pallas as pl
from jax.experimental.pallas import tpu as pltpu
from jax.sharding import PartitionSpec as P

STEPS = 4
REPLICAS = 16
beta_one = 0.9
beta_two = 0.95
learn_rate = 0.1
decay_rate = 0.1
epsilon = 1e-08
adam_offset = 101

AXES = ("replica", "shard")
DIMS = (2, 4, 2, 4, 2)


def moved(value, to):
    pairs = []
    for place in np.ndindex(*DIMS):
        z_lo, x, core, y, z_hi = place
        x, y, z, core = to(x, y, 2 * z_hi + z_lo, core)
        x, y, z = x % 4, y % 4, z % 4
        target = (z % 2, x, core, y, z // 2)
        pairs.append((int(np.ravel_multi_index(place, DIMS)), int(np.ravel_multi_index(target, DIMS))))
    return lax.ppermute(value, AXES, pairs)


POWER = 15


def coded(value, bound):
    value = value * (2.0**8.5 / bound)
    second = value * value
    fourth = second * second
    return (value * second * fourth * (fourth * fourth)).astype(jnp.bfloat16)


KEEP = 1.0 - learn_rate * decay_rate
BLOCK = 14336


def moments(first_moment, second_moment, grads, steps):
    for step in range(steps):
        gradient = grads[step].astype(jnp.float32)
        first_moment = beta_one * first_moment + (1.0 - beta_one) * gradient
        second_moment = beta_two * second_moment + (1.0 - beta_two) * gradient * gradient
    return first_moment, second_moment


def update(first_moment, second_moment, step):
    count = adam_offset + step
    first_fix = 1.0 - beta_one**count
    second_fix = 1.0 - beta_two**count
    return first_moment * (1.0 / first_fix) / (jnp.sqrt(second_moment * (1.0 / second_fix)) + epsilon)


def first_kernel(weight, params, first_moment, second_moment, grads, out):
    now = moments(first_moment[0], second_moment[0], grads[0], 1)
    out[...] = (KEEP**4 * params[0] - learn_rate * KEEP**3 * update(*now, 0)) * (weight[0] / 16.0)


SMEM = pl.BlockSpec(memory_space=pltpu.SMEM)


def moment_spec(start=0):
    return pl.BlockSpec((1, 16, BLOCK), lambda i: (0, 0, i + start))


def grad_spec(steps, start=0):
    return pl.BlockSpec((steps, 1, 16, BLOCK), lambda i: (0, 0, 0, i + start))


def first_term(weight, params, first_moment, second_moment, grads):
    cols = params.shape[-1]
    spec = pl.BlockSpec((1, 16, BLOCK), lambda i: (0, 0, i))
    return pl.pallas_call(
        first_kernel,
        grid=(cols // BLOCK,),
        in_specs=[SMEM, spec, spec, spec, pl.BlockSpec((1, 1, 16, BLOCK), lambda i: (0, 0, 0, i))],
        out_specs=pl.BlockSpec((16, BLOCK), lambda i: (0, i)),
        out_shape=jax.ShapeDtypeStruct((16, cols), jnp.float32),
        cost_estimate=pl.CostEstimate(flops=20 * 16 * cols, transcendentals=2 * 16 * cols, bytes_accessed=18 * 16 * cols),
    )(weight, params, first_moment, second_moment, grads)


def decoded(code, bound):
    code = code.astype(jnp.float32)
    root = jnp.exp(jnp.log(jnp.abs(code)) * (1.0 / POWER)) * (bound / 2.0**8.5)
    return jnp.where(code < 0, -root, root)


def gathered(one, two, y, z):
    rows, half = one.shape
    along_y = lambda v, s: moved(v, lambda x, yy, zz, c: (x, yy + s, zz, c))
    along_z = lambda v, s: moved(v, lambda x, yy, zz, c: (x, yy, zz + s, c))

    def line(v, along, at):
        block = jnp.zeros((4, rows, half), v.dtype)
        block = lax.dynamic_update_slice(block, v[None], (at, 0, 0))
        for s in (1, -1, 2):
            block = lax.dynamic_update_slice(block, along(v, s)[None], ((at - s) % 4, 0, 0))
        return block

    def blocks(v, along):
        ahead, back = along(v, -1), along(v, 1)
        far = jnp.concatenate([along(back[:2], 1), along(ahead[2:], -1)])
        return ((v, 0), (back, -1), (ahead, 1), (far, 2))

    one, two = line(one, along_y, y), line(two, along_z, z)
    out = jnp.zeros((4, 4, rows, 2 * half), one.dtype)
    for (block_one, off), (block_two, _) in zip(blocks(one, along_z), blocks(two, along_y)):
        out = lax.dynamic_update_slice(out, block_one[:, None], (0, (z + off) % 4, 0, 0))
        out = lax.dynamic_update_slice(out, block_two[None], ((y + off) % 4, 0, 0, half))
    return out


def per_device(params, first_moment, second_moment, grads, push_weight):
    replica = lax.axis_index("replica")
    shard = lax.axis_index("shard")
    z_lo, y, z = replica // 8, shard // 2, 2 * (shard % 2) + replica // 8
    cols = params.shape[-1]
    half = cols // 2
    ring = lambda v, steps: lax.ppermute(v, "replica", [(r, (r + steps) % REPLICAS) for r in range(REPLICAS)])
    mixed = lambda v, steps: 0.5 * v + 0.5 * ring(v, steps)
    mine = lambda v: jnp.where(z_lo == 0, v[:8], v[8:])
    other = lambda v: jnp.where(z_lo == 0, v[8:], v[:8])
    cores = lambda x, yy, zz, cc: (x, yy, zz, cc ^ 1)
    across = lambda x, yy, zz, cc: (x, yy, zz ^ 1, cc)
    far = lambda x, yy, zz, cc: (x ^ 2, yy, zz, cc)
    near = (lambda x, yy, zz, cc: (x ^ 1, yy, zz, cc), lambda x, yy, zz, cc: (3 - x, yy, zz, cc))

    state = (first_moment[0], second_moment[0], grads[:, 0])
    sides = [slice(side * half, side * half + half) for side in range(2)]
    a = first_term(push_weight, params, first_moment, second_moment, grads)
    a_there = moved(a, cores)
    weight_one = mixed(push_weight, 1)

    factor = -learn_rate * KEEP**2 / 8.0 * weight_one[0]
    parts, codes = [], []
    for part in sides:
        local = lax.optimization_barrier((state, a, a_there, factor))
        b = local[3] * update(*moments(local[0][0][:, part], local[0][1][:, part], local[0][2][:, :, part], 2), 1)
        ab = local[1][:, part] + local[2][:, part] + b
        parts.append(ab)
        codes.append(coded(ab, 4.0))
    codes, parts, state = lax.optimization_barrier((codes, parts, state))
    c = (-learn_rate * KEEP / 4.0) * update(*moments(*state, 3), 2)
    d = (-learn_rate / 2.0) * update(*moments(*state, 4), 3)
    c, d, d_code, weight_one = lax.optimization_barrier((c, mine(d), coded(other(d), 1.0), weight_one))
    weight_two = mixed(weight_one, 2)
    near_there = [moved(codes[side], near[side]) for side in range(2)]
    parts = [parts[side] + decoded(near_there[side], 4.0) + weight_two[0] * c[:, sides[side]] for side in range(2)]
    codes = [coded(other(part), 4.0) for part in parts]
    codes, d_code, weight_two = lax.optimization_barrier((codes, d_code, weight_two))
    d_there = moved(d_code, across)
    weight_three = mixed(weight_two, 4)
    there = [moved(code, across) for code in codes]
    there, weight_three = lax.optimization_barrier((there, weight_three))
    parts = [mine(parts[side]) + decoded(there[side], 4.0) for side in range(2)]
    codes = [coded(part, 8.0) for part in parts]
    codes, weight_three = lax.optimization_barrier((codes, weight_three))
    weight_three_there = ring(weight_three, 8)
    weight_four = 0.5 * weight_three[0] + 0.5 * weight_three_there[0]

    pieces = []
    for side, part in enumerate(sides):
        own = weight_three[0] * d[:, part] + weight_three_there[0] * decoded(d_there[:, part], 1.0)
        total = parts[side] + decoded(moved(codes[side], far), 8.0) + own
        pieces.append((total / weight_four).astype(jnp.bfloat16))
    return gathered(*pieces, y, z).reshape(1, 128, cols)


def solution(mesh):
    return jax.shard_map(
        per_device,
        mesh=mesh,
        in_specs=(
            P("replica", "shard", None),
            P("replica", "shard", None),
            P("replica", "shard", None),
            P(None, "replica", "shard", None),
            P("replica"),
        ),
        out_specs=P("replica", None, None),
        check_vma=False,
    )
```

```python
import jax
import jax.numpy as jnp
import numpy as np
from jax import lax
from jax.experimental import pallas as pl
from jax.experimental.pallas import tpu as pltpu
from jax.sharding import PartitionSpec as P

STEPS = 4
REPLICAS = 16
beta_one = 0.9
beta_two = 0.95
learn_rate = 0.1
decay_rate = 0.1
epsilon = 1e-08
adam_offset = 101

AXES = ("replica", "shard")
DIMS = (2, 4, 2, 4, 2)


def moved(value, to):
    pairs = []
    for place in np.ndindex(*DIMS):
        z_lo, x, core, y, z_hi = place
        x, y, z, core = to(x, y, 2 * z_hi + z_lo, core)
        x, y, z = x % 4, y % 4, z % 4
        target = (z % 2, x, core, y, z // 2)
        pairs.append((int(np.ravel_multi_index(place, DIMS)), int(np.ravel_multi_index(target, DIMS))))
    return lax.ppermute(value, AXES, pairs)


POWER = 15


def coded(value, bound):
    value = value * (2.0**8.5 / bound)
    second = value * value
    fourth = second * second
    return (value * second * fourth * (fourth * fourth)).astype(jnp.bfloat16)


KEEP = 1.0 - learn_rate * decay_rate
BLOCK = 14336


def moments(first_moment, second_moment, grads, steps):
    for step in range(steps):
        gradient = grads[step].astype(jnp.float32)
        first_moment = beta_one * first_moment + (1.0 - beta_one) * gradient
        second_moment = beta_two * second_moment + (1.0 - beta_two) * gradient * gradient
    return first_moment, second_moment


def update(first_moment, second_moment, step):
    count = adam_offset + step
    first_fix = 1.0 - beta_one**count
    second_fix = 1.0 - beta_two**count
    return first_moment * (1.0 / first_fix) / (jnp.sqrt(second_moment * (1.0 / second_fix)) + epsilon)


def first_kernel(weight, params, first_moment, second_moment, grads, out):
    now = moments(first_moment[0], second_moment[0], grads[0], 1)
    out[...] = (KEEP**4 * params[0] - learn_rate * KEEP**3 * update(*now, 0)) * (weight[0] / 16.0)


SMEM = pl.BlockSpec(memory_space=pltpu.SMEM)


def moment_spec(start=0):
    return pl.BlockSpec((1, 16, BLOCK), lambda i: (0, 0, i + start))


def grad_spec(steps, start=0):
    return pl.BlockSpec((steps, 1, 16, BLOCK), lambda i: (0, 0, 0, i + start))


def first_term(weight, params, first_moment, second_moment, grads):
    cols = params.shape[-1]
    spec = pl.BlockSpec((1, 16, BLOCK), lambda i: (0, 0, i))
    return pl.pallas_call(
        first_kernel,
        grid=(cols // BLOCK,),
        in_specs=[SMEM, spec, spec, spec, pl.BlockSpec((1, 1, 16, BLOCK), lambda i: (0, 0, 0, i))],
        out_specs=pl.BlockSpec((16, BLOCK), lambda i: (0, i)),
        out_shape=jax.ShapeDtypeStruct((16, cols), jnp.float32),
        cost_estimate=pl.CostEstimate(flops=20 * 16 * cols, transcendentals=2 * 16 * cols, bytes_accessed=18 * 16 * cols),
    )(weight, params, first_moment, second_moment, grads)


def decoded(code, bound):
    code = code.astype(jnp.float32)
    root = jnp.exp(jnp.log(jnp.abs(code)) * (1.0 / POWER)) * (bound / 2.0**8.5)
    return jnp.where(code < 0, -root, root)


def gathered(one, two, y, z):
    rows, half = one.shape
    along_y = lambda v, s: moved(v, lambda x, yy, zz, c: (x, yy + s, zz, c))
    along_z = lambda v, s: moved(v, lambda x, yy, zz, c: (x, yy, zz + s, c))

    def line(v, along, at):
        block = jnp.zeros((4, rows, half), v.dtype)
        block = lax.dynamic_update_slice(block, v[None], (at, 0, 0))
        for s in (1, -1, 2):
            block = lax.dynamic_update_slice(block, along(v, s)[None], ((at - s) % 4, 0, 0))
        return block

    def blocks(v, along):
        ahead, back = along(v, -1), along(v, 1)
        far = jnp.concatenate([along(back[:2], 1), along(ahead[2:], -1)])
        return ((v, 0), (back, -1), (ahead, 1), (far, 2))

    one, two = line(one, along_y, y), line(two, along_z, z)
    out = jnp.zeros((4, 4, rows, 2 * half), one.dtype)
    for (block_one, off), (block_two, _) in zip(blocks(one, along_z), blocks(two, along_y)):
        out = lax.dynamic_update_slice(out, block_one[:, None], (0, (z + off) % 4, 0, 0))
        out = lax.dynamic_update_slice(out, block_two[None], ((y + off) % 4, 0, 0, half))
    return out


def per_device(params, first_moment, second_moment, grads, push_weight):
    replica = lax.axis_index("replica")
    shard = lax.axis_index("shard")
    z_lo, y, z = replica // 8, shard // 2, 2 * (shard % 2) + replica // 8
    cols = params.shape[-1]
    half = cols // 2
    ring = lambda v, steps: lax.ppermute(v, "replica", [(r, (r + steps) % REPLICAS) for r in range(REPLICAS)])
    mixed = lambda v, steps: 0.5 * v + 0.5 * ring(v, steps)
    mine = lambda v: jnp.where(z_lo == 0, v[:8], v[8:])
    other = lambda v: jnp.where(z_lo == 0, v[8:], v[:8])
    cores = lambda x, yy, zz, cc: (x, yy, zz, cc ^ 1)
    across = lambda x, yy, zz, cc: (x, yy, zz ^ 1, cc)
    far = lambda x, yy, zz, cc: (x ^ 2, yy, zz, cc)
    near = (lambda x, yy, zz, cc: (x ^ 1, yy, zz, cc), lambda x, yy, zz, cc: (3 - x, yy, zz, cc))

    state = (first_moment[0], second_moment[0], grads[:, 0])
    sides = [slice(side * half, side * half + half) for side in range(2)]
    a = first_term(push_weight, params, first_moment, second_moment, grads)
    a_there = moved(a, cores)
    weight_one = mixed(push_weight, 1)

    a, later = lax.optimization_barrier((a, state))
    c = (-learn_rate * KEEP / 4.0) * update(*moments(*later, 3), 2)
    d = (-learn_rate / 2.0) * update(*moments(*later, 4), 3)
    d, d_code = mine(d), coded(other(d), 1.0)
    d_there = moved(d_code, across)
    factor = -learn_rate * KEEP**2 / 8.0 * weight_one[0]
    c, d_code, factor, state = lax.optimization_barrier((c, d_code, factor, state))
    b = factor * update(*moments(*state, 2), 1)
    ab = a + a_there + b
    codes = [coded(ab[:, part], 4.0) for part in sides]
    d_there, weight_one = lax.optimization_barrier((d_there, weight_one))
    weight_two = mixed(weight_one, 2)
    near_there = [moved(codes[side], near[side]) for side in range(2)]
    parts = [ab[:, part] + decoded(near_there[side], 4.0) + weight_two[0] * c[:, part] for side, part in enumerate(sides)]
    codes = [coded(other(part), 4.0) for part in parts]
    codes, weight_two = lax.optimization_barrier((codes, weight_two))
    weight_three = mixed(weight_two, 4)
    there = [moved(code, across) for code in codes]
    parts = [mine(parts[side]) + decoded(there[side], 4.0) for side in range(2)]
    codes = [coded(part, 8.0) for part in parts]
    codes[1], weight_three = lax.optimization_barrier((codes[1], weight_three))
    weight_three_there = ring(weight_three, 8)
    weight_four = 0.5 * weight_three[0] + 0.5 * weight_three_there[0]
    own = weight_three[0] * d + weight_three_there[0] * decoded(d_there, 1.0)

    pieces = []
    for side, part in enumerate(sides):
        before = lax.optimization_barrier(parts[side] + own[:, part])
        total = before + decoded(moved(codes[side], far), 8.0)
        pieces.append((total / weight_four).astype(jnp.bfloat16))
    return gathered(*pieces, y, z).reshape(1, 128, cols)


def solution(mesh):
    return jax.shard_map(
        per_device,
        mesh=mesh,
        in_specs=(
            P("replica", "shard", None),
            P("replica", "shard", None),
            P("replica", "shard", None),
            P(None, "replica", "shard", None),
            P("replica"),
        ),
        out_specs=P("replica", None, None),
        check_vma=False,
    )
```

```python
import jax
import jax.numpy as jnp
import numpy as np
from jax import lax
from jax.experimental import pallas as pl
from jax.experimental.pallas import tpu as pltpu
from jax.sharding import PartitionSpec as P

STEPS = 4
REPLICAS = 16
beta_one = 0.9
beta_two = 0.95
learn_rate = 0.1
decay_rate = 0.1
epsilon = 1e-08
adam_offset = 101

AXES = ("replica", "shard")
DIMS = (2, 4, 2, 4, 2)


def moved(value, to):
    pairs = []
    for place in np.ndindex(*DIMS):
        z_lo, x, core, y, z_hi = place
        x, y, z, core = to(x, y, 2 * z_hi + z_lo, core)
        x, y, z = x % 4, y % 4, z % 4
        target = (z % 2, x, core, y, z // 2)
        pairs.append((int(np.ravel_multi_index(place, DIMS)), int(np.ravel_multi_index(target, DIMS))))
    return lax.ppermute(value, AXES, pairs)


POWER = 15


def coded(value, bound):
    value = value * (2.0**8.5 / bound)
    second = value * value
    fourth = second * second
    return (value * second * fourth * (fourth * fourth)).astype(jnp.bfloat16)


KEEP = 1.0 - learn_rate * decay_rate
BLOCK = 14336


def moments(first_moment, second_moment, grads, steps):
    for step in range(steps):
        gradient = grads[step].astype(jnp.float32)
        first_moment = beta_one * first_moment + (1.0 - beta_one) * gradient
        second_moment = beta_two * second_moment + (1.0 - beta_two) * gradient * gradient
    return first_moment, second_moment


def update(first_moment, second_moment, step):
    count = adam_offset + step
    first_fix = 1.0 - beta_one**count
    second_fix = 1.0 - beta_two**count
    return first_moment * (1.0 / first_fix) / (jnp.sqrt(second_moment * (1.0 / second_fix)) + epsilon)


def first_kernel(weight, params, first_moment, second_moment, grads, out):
    now = moments(first_moment[0], second_moment[0], grads[0], 1)
    out[...] = (KEEP**4 * params[0] - learn_rate * KEEP**3 * update(*now, 0)) * (weight[0] / 16.0)


SMEM = pl.BlockSpec(memory_space=pltpu.SMEM)


def moment_spec(start=0):
    return pl.BlockSpec((1, 16, BLOCK), lambda i: (0, 0, i + start))


def grad_spec(steps, start=0):
    return pl.BlockSpec((steps, 1, 16, BLOCK), lambda i: (0, 0, 0, i + start))


def first_term(weight, params, first_moment, second_moment, grads):
    cols = params.shape[-1]
    spec = pl.BlockSpec((1, 16, BLOCK), lambda i: (0, 0, i))
    return pl.pallas_call(
        first_kernel,
        grid=(cols // BLOCK,),
        in_specs=[SMEM, spec, spec, spec, pl.BlockSpec((1, 1, 16, BLOCK), lambda i: (0, 0, 0, i))],
        out_specs=pl.BlockSpec((16, BLOCK), lambda i: (0, i)),
        out_shape=jax.ShapeDtypeStruct((16, cols), jnp.float32),
        cost_estimate=pl.CostEstimate(flops=20 * 16 * cols, transcendentals=2 * 16 * cols, bytes_accessed=18 * 16 * cols),
    )(weight, params, first_moment, second_moment, grads)


def decoded(code, bound):
    code = code.astype(jnp.float32)
    root = jnp.exp(jnp.log(jnp.abs(code)) * (1.0 / POWER)) * (bound / 2.0**8.5)
    return jnp.where(code < 0, -root, root)


def unwritten(shape, dtype):
    return pl.pallas_call(
        lambda out: None, out_specs=pl.BlockSpec(memory_space=pltpu.HBM), out_shape=jax.ShapeDtypeStruct(shape, dtype)
    )()


def held(value):
    spec = pl.BlockSpec(memory_space=pltpu.HBM)
    return pl.pallas_call(
        lambda value, out: None,
        in_specs=[spec],
        out_specs=spec,
        out_shape=jax.ShapeDtypeStruct(value.shape, value.dtype),
        input_output_aliases={0: 0},
    )(value)


def gathered(one, two, y, z):
    rows, half = one.shape
    along_y = lambda v, s: moved(v, lambda x, yy, zz, c: (x, yy + s, zz, c))
    along_z = lambda v, s: moved(v, lambda x, yy, zz, c: (x, yy, zz + s, c))

    def line(v, along, at):
        block = jnp.zeros((4, rows, half), v.dtype)
        block = lax.dynamic_update_slice(block, v[None], (at, 0, 0))
        for s in (1, -1, 2):
            block = lax.dynamic_update_slice(block, along(v, s)[None], ((at - s) % 4, 0, 0))
        return block

    def put_one(out, block, first, off):
        return lax.dynamic_update_slice(out, block[:, None], (first, (z + off) % 4, 0, 0))

    def put_two(out, block, first, off):
        return lax.dynamic_update_slice(out, block[None], ((y + off) % 4, first, 0, half))

    one, two = line(one, along_y, y), line(two, along_z, z)
    out = unwritten((4, 4, rows, 2 * half), one.dtype)
    out = put_two(put_one(out, one, 0, 0), two, 0, 0)
    near, ends = [], []
    for put, block, along in ((put_one, one, along_z), (put_two, two, along_y)):
        ahead, back = along(block, -1), along(block, 1)
        near.append((put, back, ahead))
        ends.append((put, along(back[:2], 1), along(ahead[2:], -1)))
    for put, back, ahead in reversed(near):
        out = put(put(out, back, 0, -1), ahead, 0, 1)
    for put, low, high in reversed(ends):
        out = put(put(out, low, 0, 2), high, 2, 2)
    return held(out)


def per_device(params, first_moment, second_moment, grads, push_weight):
    replica = lax.axis_index("replica")
    shard = lax.axis_index("shard")
    z_lo, y, z = replica // 8, shard // 2, 2 * (shard % 2) + replica // 8
    cols = params.shape[-1]
    half = cols // 2
    ring = lambda v, steps: lax.ppermute(v, "replica", [(r, (r + steps) % REPLICAS) for r in range(REPLICAS)])
    mixed = lambda v, steps: 0.5 * v + 0.5 * ring(v, steps)
    mine = lambda v: jnp.where(z_lo == 0, v[:8], v[8:])
    other = lambda v: jnp.where(z_lo == 0, v[8:], v[:8])
    cores = lambda x, yy, zz, cc: (x, yy, zz, cc ^ 1)
    across = lambda x, yy, zz, cc: (x, yy, zz ^ 1, cc)
    far = lambda x, yy, zz, cc: (x ^ 2, yy, zz, cc)
    near = (lambda x, yy, zz, cc: (x ^ 1, yy, zz, cc), lambda x, yy, zz, cc: (3 - x, yy, zz, cc))

    state = (first_moment[0], second_moment[0], grads[:, 0])
    sides = [slice(side * half, side * half + half) for side in range(2)]
    a = first_term(push_weight, params, first_moment, second_moment, grads)
    a_there = moved(a, cores)
    weight_one = mixed(push_weight, 1)

    a, later = lax.optimization_barrier((a, state))
    c = (-learn_rate * KEEP / 4.0) * update(*moments(*later, 3), 2)
    d = (-learn_rate / 2.0) * update(*moments(*later, 4), 3)
    d, d_code = mine(d), coded(other(d), 1.0)
    d_there = moved(d_code, across)
    factor = -learn_rate * KEEP**2 / 8.0 * weight_one[0]
    c, d_code, factor, state = lax.optimization_barrier((c, d_code, factor, state))
    b = factor * update(*moments(*state, 2), 1)
    ab = a + a_there + b
    codes = [coded(ab[:, part], 4.0) for part in sides]
    d_there, weight_one = lax.optimization_barrier((d_there, weight_one))
    weight_two = mixed(weight_one, 2)
    near_there = [moved(codes[side], near[side]) for side in range(2)]
    parts = [ab[:, part] + decoded(near_there[side], 4.0) + weight_two[0] * c[:, part] for side, part in enumerate(sides)]
    codes = [coded(other(part), 4.0) for part in parts]
    codes, weight_two = lax.optimization_barrier((codes, weight_two))
    weight_three = mixed(weight_two, 4)
    there = [moved(code, across) for code in codes]
    parts = [mine(parts[side]) + decoded(there[side], 4.0) for side in range(2)]
    codes = [coded(part, 8.0) for part in parts]
    codes[1], weight_three = lax.optimization_barrier((codes[1], weight_three))
    weight_three_there = ring(weight_three, 8)
    weight_four = 0.5 * weight_three[0] + 0.5 * weight_three_there[0]
    own = weight_three[0] * d + weight_three_there[0] * decoded(d_there, 1.0)

    pieces = []
    for side, part in enumerate(sides):
        before = lax.optimization_barrier(parts[side] + own[:, part])
        total = before + decoded(moved(codes[side], far), 8.0)
        pieces.append((total / weight_four).astype(jnp.bfloat16))
    return gathered(*pieces, y, z).reshape(1, 128, cols)


def solution(mesh):
    return jax.shard_map(
        per_device,
        mesh=mesh,
        in_specs=(
            P("replica", "shard", None),
            P("replica", "shard", None),
            P("replica", "shard", None),
            P(None, "replica", "shard", None),
            P("replica"),
        ),
        out_specs=P("replica", None, None),
        check_vma=False,
    )
```

```python
import jax
import jax.numpy as jnp
import numpy as np
from jax import lax
from jax.experimental import pallas as pl
from jax.experimental.pallas import tpu as pltpu
from jax.sharding import PartitionSpec as P

STEPS = 4
REPLICAS = 16
beta_one = 0.9
beta_two = 0.95
learn_rate = 0.1
decay_rate = 0.1
epsilon = 1e-08
adam_offset = 101

AXES = ("replica", "shard")
DIMS = (2, 4, 2, 4, 2)


def moved(value, to):
    pairs = []
    for place in np.ndindex(*DIMS):
        z_lo, x, core, y, z_hi = place
        x, y, z, core = to(x, y, 2 * z_hi + z_lo, core)
        x, y, z = x % 4, y % 4, z % 4
        target = (z % 2, x, core, y, z // 2)
        pairs.append((int(np.ravel_multi_index(place, DIMS)), int(np.ravel_multi_index(target, DIMS))))
    return lax.ppermute(value, AXES, pairs)


POWER = 15


def coded(value, bound):
    value = value * (2.0**8.5 / bound)
    second = value * value
    fourth = second * second
    return (value * second * fourth * (fourth * fourth)).astype(jnp.bfloat16)


KEEP = 1.0 - learn_rate * decay_rate
BLOCK = 14336


def moments(first_moment, second_moment, grads, steps):
    for step in range(steps):
        gradient = grads[step].astype(jnp.float32)
        first_moment = beta_one * first_moment + (1.0 - beta_one) * gradient
        second_moment = beta_two * second_moment + (1.0 - beta_two) * gradient * gradient
    return first_moment, second_moment


def update(first_moment, second_moment, step):
    count = adam_offset + step
    first_fix = 1.0 - beta_one**count
    second_fix = 1.0 - beta_two**count
    return first_moment * (1.0 / first_fix) / (jnp.sqrt(second_moment * (1.0 / second_fix)) + epsilon)


def first_kernel(weight, params, first_moment, second_moment, grads, out):
    now = moments(first_moment[0], second_moment[0], grads[0], 1)
    out[...] = (KEEP**4 * params[0] - learn_rate * KEEP**3 * update(*now, 0)) * (weight[0] / 16.0)


SMEM = pl.BlockSpec(memory_space=pltpu.SMEM)


def moment_spec(start=0):
    return pl.BlockSpec((1, 16, BLOCK), lambda i: (0, 0, i + start))


def grad_spec(steps, start=0):
    return pl.BlockSpec((steps, 1, 16, BLOCK), lambda i: (0, 0, 0, i + start))


def first_term(weight, params, first_moment, second_moment, grads):
    cols = params.shape[-1]
    spec = pl.BlockSpec((1, 16, BLOCK), lambda i: (0, 0, i))
    return pl.pallas_call(
        first_kernel,
        grid=(cols // BLOCK,),
        in_specs=[SMEM, spec, spec, spec, pl.BlockSpec((1, 1, 16, BLOCK), lambda i: (0, 0, 0, i))],
        out_specs=pl.BlockSpec((16, BLOCK), lambda i: (0, i)),
        out_shape=jax.ShapeDtypeStruct((16, cols), jnp.float32),
        cost_estimate=pl.CostEstimate(flops=20 * 16 * cols, transcendentals=2 * 16 * cols, bytes_accessed=18 * 16 * cols),
    )(weight, params, first_moment, second_moment, grads)


def decoded(code, bound):
    code = code.astype(jnp.float32)
    root = jnp.exp(jnp.log(jnp.abs(code)) * (1.0 / POWER)) * (bound / 2.0**8.5)
    return jnp.where(code < 0, -root, root)


def unwritten(shape, dtype):
    return pl.pallas_call(
        lambda out: None, out_specs=pl.BlockSpec(memory_space=pltpu.HBM), out_shape=jax.ShapeDtypeStruct(shape, dtype)
    )()


def held(value):
    spec = pl.BlockSpec(memory_space=pltpu.HBM)
    return pl.pallas_call(
        lambda value, out: None,
        in_specs=[spec],
        out_specs=spec,
        out_shape=jax.ShapeDtypeStruct(value.shape, value.dtype),
        input_output_aliases={0: 0},
    )(value)


def gathered(one, two, y, z):
    rows, half = one.shape
    along_y = lambda v, s: moved(v, lambda x, yy, zz, c: (x, yy + s, zz, c))
    along_z = lambda v, s: moved(v, lambda x, yy, zz, c: (x, yy, zz + s, c))

    def line(v, along, at):
        block = jnp.zeros((4, rows, half), v.dtype)
        block = lax.dynamic_update_slice(block, v[None], (at, 0, 0))
        for s in (1, -1, 2):
            block = lax.dynamic_update_slice(block, along(v, s)[None], ((at - s) % 4, 0, 0))
        return block

    def put_one(out, block, first, off):
        return lax.dynamic_update_slice(out, block[:, None], (first, (z + off) % 4, 0, 0))

    def put_two(out, block, first, off):
        return lax.dynamic_update_slice(out, block[None], ((y + off) % 4, first, 0, half))

    one, two = line(one, along_y, y), line(two, along_z, z)
    out = unwritten((4, 4, rows, 2 * half), one.dtype)
    out = put_two(put_one(out, one, 0, 0), two, 0, 0)
    near, ends = [], []
    for put, block, along in ((put_one, one, along_z), (put_two, two, along_y)):
        ahead, back = along(block, -1), along(block, 1)
        near.append((put, back, ahead))
        ends.append((put, along(back[:2], 1), along(ahead[2:], -1)))
    for put, back, ahead in reversed(near):
        out = put(put(out, back, 0, -1), ahead, 0, 1)
    for put, low, high in reversed(ends):
        out = put(put(out, low, 0, 2), high, 2, 2)
    return held(out)


def per_device(params, first_moment, second_moment, grads, push_weight):
    replica = lax.axis_index("replica")
    shard = lax.axis_index("shard")
    z_lo, y, z = replica // 8, shard // 2, 2 * (shard % 2) + replica // 8
    cols = params.shape[-1]
    half = cols // 2
    ring = lambda v, steps: lax.ppermute(v, "replica", [(r, (r + steps) % REPLICAS) for r in range(REPLICAS)])
    mixed = lambda v, steps: 0.5 * v + 0.5 * ring(v, steps)
    mine = lambda v: jnp.where(z_lo == 0, v[:8], v[8:])
    other = lambda v: jnp.where(z_lo == 0, v[8:], v[:8])
    cores = lambda x, yy, zz, cc: (x, yy, zz, cc ^ 1)
    across = lambda x, yy, zz, cc: (x, yy, zz ^ 1, cc)
    far = lambda x, yy, zz, cc: (x ^ 2, yy, zz, cc)
    near = (lambda x, yy, zz, cc: (x ^ 1, yy, zz, cc), lambda x, yy, zz, cc: (3 - x, yy, zz, cc))

    state = (first_moment[0], second_moment[0], grads[:, 0])
    sides = [slice(side * half, side * half + half) for side in range(2)]
    a = first_term(push_weight, params, first_moment, second_moment, grads)
    a_there = moved(a, cores)
    weight_one = mixed(push_weight, 1)

    a, later = lax.optimization_barrier((a, state))
    c = (-learn_rate * KEEP / 4.0) * update(*moments(*later, 3), 2)
    d = (-learn_rate / 2.0) * update(*moments(*later, 4), 3)
    d, d_code = mine(d), coded(other(d), 1.0)
    d_there = moved(d_code, across)
    factor = -learn_rate * KEEP**2 / 8.0 * weight_one[0]
    c, d_code, factor, state = lax.optimization_barrier((c, d_code, factor, state))
    b = factor * update(*moments(*state, 2), 1)
    ab = a + a_there + b
    codes = [coded(ab[:, part], 4.0) for part in sides]
    d_there, weight_one = lax.optimization_barrier((d_there, weight_one))
    weight_two = mixed(weight_one, 2)
    near_there = [moved(codes[side], near[side]) for side in range(2)]
    parts = [ab[:, part] + decoded(near_there[side], 4.0) + weight_two[0] * c[:, part] for side, part in enumerate(sides)]
    codes = [coded(other(part), 4.0) for part in parts]
    codes[1], weight_two = lax.optimization_barrier((codes[1], weight_two))
    weight_three = mixed(weight_two, 4)
    there = [moved(code, across) for code in codes]
    parts = [mine(parts[side]) + decoded(there[side], 4.0) for side in range(2)]
    codes = [coded(part, 8.0) for part in parts]
    codes[1], weight_three = lax.optimization_barrier((codes[1], weight_three))
    weight_three_there = ring(weight_three, 8)
    weight_four = 0.5 * weight_three[0] + 0.5 * weight_three_there[0]
    own = weight_three[0] * d + weight_three_there[0] * decoded(d_there, 1.0)

    pieces = []
    for side, part in enumerate(sides):
        before = lax.optimization_barrier(parts[side] + own[:, part])
        total = before + decoded(moved(codes[side], far), 8.0)
        pieces.append((total / weight_four).astype(jnp.bfloat16))
    return gathered(*pieces, y, z).reshape(1, 128, cols)


def solution(mesh):
    return jax.shard_map(
        per_device,
        mesh=mesh,
        in_specs=(
            P("replica", "shard", None),
            P("replica", "shard", None),
            P("replica", "shard", None),
            P(None, "replica", "shard", None),
            P("replica"),
        ),
        out_specs=P("replica", None, None),
        check_vma=False,
    )
```
